32 devices in a mesh: dp: 8 (over z, y), seq: 4 (over x, core).
Axes of the slice: x: 2, y: 2, z: 4, core: 2. Of those that a mesh axis runs over, the one named last changes fastest.
Arguments:
- hidden_states: bfloat16 [4096, 2048], P(('dp', 'seq'))
- query_weight: bfloat16 [2048, 512], P('dp')
- key_weight: bfloat16 [2048, 128], P('dp')
- value_weight: bfloat16 [2048, 128], P('dp'), may hold values from -0.125 to 0.125
- doc_lengths: int32 [8, 8], P('dp'), may hold values from 1 to 256, 512 in all within a row
Outputs:
- context: bfloat16 [4096, 512], P(('dp', 'seq'))
The draws below stay inside these ranges and needn't reach their ends.
Inputs may be any that keep to these rules, and one draw needn't show every extreme that they name: `doc_lengths`: each row sums to 512, and its longest document has exactly 256 tokens.
All inputs are finite; a program needn't handle non-finite values.
Results may differ from the reference program's by a relative error of at most 0.0076.
Values may be sent and summed in bfloat16 or wider, within the bound.
A program may use at most 64 MiB of HBM per device.

```python
import math
import jax
import jax.numpy as jnp
import numpy as np
from jax import lax

D = 2048
HD = 64
DOCS = 8
H = 8
KVH = 2
SEQLEN = 512
TOKENS = 4096
N_DP = 8


def paired_weights(key):
    first_key, second_key = jax.random.split(jax.random.fold_in(key, 7), 2)
    key_part = jnp.clip(jax.random.normal(first_key, (D, KVH * HD), jnp.float32), -4.0, 4.0) / math.sqrt(D)
    noise = jnp.clip(jax.random.normal(second_key, (D, H * HD), jnp.float32), -4.0, 4.0) / math.sqrt(D)
    query_part = noise
    return (query_part, key_part)


def draw_query_weight(key, part):
    return paired_weights(key)[0].astype(jnp.bfloat16)


def draw_key_weight(key, part):
    return paired_weights(key)[1].astype(jnp.bfloat16)


def draw_hidden_states(key, part):
    first_key, second_key, third_key = jax.random.split(jax.random.fold_in(key, 11), 3)
    entries = jnp.clip(jax.random.normal(first_key, (TOKENS, D), jnp.float32), -4.0, 4.0)
    columns = jnp.exp(jax.random.uniform(second_key, (1, D), jnp.float32) * math.log(10.0))
    rows_scale = jnp.exp(jax.random.uniform(third_key, (TOKENS, 1), jnp.float32) * math.log(10.0))
    return (entries * columns * rows_scale).astype(jnp.bfloat16)


def levels(key, shape, cuts, least, top_value):
    loudness = 1.0
    for position, shards_of in cuts:
        steps = jax.random.uniform(jax.random.fold_in(jax.random.fold_in(key, 6), position), (shards_of,), jnp.float32, least / len(cuts), top_value / len(cuts))
        loudness = loudness * jnp.repeat(jnp.exp(steps), shape[position] // shards_of).reshape((-1,) + (1,) * (len(shape) - 1 - position))
    return loudness


def split_up(amount, total, most, skew):
    portions = [(1 << 20) // math.isqrt(grade ** skew) + 1 for grade in range(2, amount + 1)]
    rest, given = total - most - (amount - 1), [1] * (amount - 1)
    while rest > 0:
        free = [i for i in range(amount - 1) if given[i] < most]
        whole, left = sum([portions[i] for i in free]), rest
        for i in free:
            more = min(most - given[i], max(1, left * portions[i] // whole), rest)
            given[i] = given[i] + more
            rest = rest - more
    return np.array([most] + given)


def ragged_sizes(rng, amount, total, reach, lean):
    if amount == 2:
        one = jax.random.randint(rng, (), max(1, total - reach), min(reach, total - 1) + 1)
        return jnp.stack([one, total - one])
    tallies = jnp.asarray(split_up(amount, total, reach, lean), jnp.int32)
    couples = (amount - 1) // 2
    giver, sink = tallies[1:1 + 2 * couples:2], tallies[2:2 + 2 * couples:2]
    room = jnp.minimum(giver - 1, reach - sink)
    moved = jax.random.randint(jax.random.fold_in(rng, 1), (couples,), 0, 1 << 20) % (room + 1)
    tallies = tallies.at[1:1 + 2 * couples:2].set(giver - moved).at[2:2 + 2 * couples:2].set(sink + moved)
    return tallies[jax.random.permutation(jax.random.fold_in(rng, 2), amount)]


def normal_values(rng, extent, scale, most, cuts=(), held_as=jnp.bfloat16):
    values = scale * jax.random.normal(rng, extent, jnp.float32)
    if cuts:
        values = values * levels(rng, extent, cuts, -0.22, 0.18)
    return jnp.clip(values, -most, most).astype(held_as)


def setup_inputs(seed: int = 0) -> dict:
    streams_of = jax.random.split(jax.random.key(seed), 6)
    hidden_states = draw_hidden_states(jax.random.fold_in(streams_of[5], 71), 0)
    query_weight = draw_query_weight(jax.random.fold_in(streams_of[5], 71), 0)
    key_weight = draw_key_weight(jax.random.fold_in(streams_of[5], 71), 0)
    value_weight = normal_values(streams_of[3], (D, KVH * HD), D ** -0.5, 0.125, ((0, 8),))
    doc_lengths = jax.vmap(lambda own: ragged_sizes(own, DOCS, SEQLEN, SEQLEN // 2, 2))(jax.random.split(streams_of[4], N_DP)).reshape((N_DP, DOCS)).astype(jnp.int32)
    return {"hidden_states": hidden_states, "query_weight": query_weight, "key_weight": key_weight, "value_weight": value_weight, "doc_lengths": doc_lengths}


EPSILON = 1e-05
THETA = 500000.0
NEG_FILL = -1e+30

def normalize(states):
    floats = states.astype(jnp.float32)
    scale = lax.rsqrt(lax.optimization_barrier(jnp.mean(floats * floats, axis=-1, keepdims=True)) + EPSILON)
    return (floats * scale).astype(jnp.bfloat16)

def doc_offsets(doc_sizes, positions):
    ends = jnp.cumsum(doc_sizes).astype(jnp.int32)
    before = (ends[None, :] <= positions[:, None]).astype(jnp.int32)
    docs = lax.optimization_barrier(jnp.sum(before, axis=1)).astype(jnp.int32)
    starts = lax.optimization_barrier(jnp.sum(before * doc_sizes[None, :], axis=1)).astype(jnp.int32)
    return (docs, positions - starts)

def rotate(vectors, offset):
    half_dim = vectors.shape[-1] // 2
    index = jnp.arange(half_dim, dtype=jnp.float32)
    freqs = jnp.exp(index * (-2.0 / vectors.shape[-1]) * math.log(THETA))
    angle = offset.astype(jnp.float32)[:, None] * freqs[None, :]
    cosine = jnp.cos(angle)[:, None, :]
    sine = jnp.sin(angle)[:, None, :]
    first = vectors[..., :half_dim]
    second = vectors[..., half_dim:]
    return jnp.concatenate([first * cosine - second * sine, second * cosine + first * sine], axis=-1)

def attend(queries, keys, values, docs):
    seq_length = queries.shape[0]
    group = queries.shape[1]
    scale = queries.shape[-1] ** (-0.5)
    block = math.gcd(256, seq_length)
    key_pos = jnp.arange(seq_length, dtype=jnp.int32)

    def one_block(number):
        first_row = number * block
        query_block = lax.dynamic_slice_in_dim(queries, first_row, block, 0)
        query_docs = lax.dynamic_slice_in_dim(docs, first_row, block, 0)
        query_pos = first_row + jnp.arange(block, dtype=jnp.int32)
        scores = jnp.einsum('qgd,kd->gqk', query_block.astype(jnp.float32), keys.astype(jnp.float32)) * scale
        allowed = (key_pos[None, :] <= query_pos[:, None]) & (docs[None, :] == query_docs[:, None])
        scores = jnp.where(allowed[None], scores, NEG_FILL)
        highest = lax.optimization_barrier(jnp.max(scores, axis=-1, keepdims=True))
        expons = jnp.exp(scores - highest)
        totals = lax.optimization_barrier(jnp.sum(expons, axis=-1, keepdims=True))
        weights = (expons / totals).astype(jnp.bfloat16)
        mixed = jnp.einsum('gqk,kd->qgd', weights.astype(jnp.float32), values.astype(jnp.float32))
        return mixed.astype(jnp.bfloat16)
    blocks = lax.map(one_block, jnp.arange(seq_length // block, dtype=jnp.int32))
    return blocks.reshape(seq_length, group * queries.shape[-1])

def reference(hidden_states, query_weight, key_weight, value_weight, doc_lengths):
    group = H // KVH

    def one_sequence(packed):
        states, doc_sizes = packed
        normed = normalize(states)
        query_lin = jnp.dot(normed, query_weight, preferred_element_type=jnp.float32)
        key_lin = jnp.dot(normed, key_weight, preferred_element_type=jnp.float32)
        value_lin = jnp.dot(normed, value_weight, preferred_element_type=jnp.float32)
        positions = jnp.arange(SEQLEN, dtype=jnp.int32)
        docs, offset = doc_offsets(doc_sizes, positions)
        queries = rotate(query_lin.reshape(SEQLEN, H, HD), offset).astype(jnp.bfloat16)
        keys = rotate(key_lin.reshape(SEQLEN, KVH, HD), offset).astype(jnp.bfloat16)
        values = value_lin.astype(jnp.bfloat16).reshape(SEQLEN, KVH, HD)
        grouped = queries.reshape(SEQLEN, KVH, group, HD).transpose(1, 0, 2, 3)

        def one_head(item):
            return attend(item[0], item[1], item[2], docs)
        heads_out = lax.map(one_head, (grouped, keys.transpose(1, 0, 2), values.transpose(1, 0, 2)))
        return heads_out.transpose(1, 0, 2).reshape(SEQLEN, H * HD)
    outputs = lax.map(one_sequence, (hidden_states.reshape(N_DP, SEQLEN, D), doc_lengths))
    return outputs.reshape(TOKENS, H * HD)
```

```python
import functools
import math

import jax
import jax.numpy as jnp
from jax import lax
from jax.experimental import pallas as pl
from jax.experimental.pallas import tpu as pltpu
from jax.sharding import PartitionSpec as P

HD = 64
GROUP = 4
LANES = 128
INNER = 2
CORES = 2
PIECES = 4
EPSILON = 1e-05
THETA = 500000.0
NEG_FILL = -1e30
MESH = pl.DeviceIdType.MESH


def kernel(n_dp, n_seq, docs, h_ref, q_ref, k_ref, v_ref, len_ref, out_ref,
           hid, nrm, wbuf, kraw, vraw, cos_buf, sin_buf, bias, qs, ks, v0, v1, ctx,
           loc_sem, hs_sem, hf_sem, hc_sem, hr_sem, ws_sem, wr_sem, os_sem, or_sem):
    dp = lax.axis_index("dp")
    me = lax.axis_index("seq")
    tok, depth = h_ref.shape
    kd = q_ref.shape[0]
    length = tok * n_seq
    n_z = n_dp // INNER
    n_x = n_seq // CORES
    z, y = dp // INNER, dp % INNER
    x, core = me // CORES, me % CORES
    mate = x * CORES + (1 - core)
    rows = tok // PIECES
    kv_head = (me * (LANES // HD)) // GROUP
    kv_block = pl.multiple_of((kv_head * HD // LANES) * LANES, LANES)
    kv_odd = (kv_head * HD // LANES) * LANES != kv_head * HD
    window = length // 2

    def dev(d, s):
        return {"dp": d, "seq": s}

    def own_rows(index):
        return pl.ds(pl.multiple_of(index * kd, kd), kd)

    q_cols = pl.ds(pl.multiple_of(me * LANES, LANES), LANES)
    local = [
        pltpu.make_async_copy(k_ref.at[:, pl.ds(kv_block, LANES)], kraw, loc_sem.at[0]),
        pltpu.make_async_copy(v_ref.at[:, pl.ds(kv_block, LANES)], vraw, loc_sem.at[1]),
        pltpu.make_async_copy(q_ref.at[:, q_cols], wbuf.at[own_rows(dp), pl.ds(0, LANES)], loc_sem.at[2]),
        pltpu.make_async_copy(h_ref, hid.at[me], loc_sem.at[3]),
    ]
    for copy in local:
        copy.start()

    has_left, has_right = z > 0, z < n_z - 1
    left, right, across = dp - INNER, dp + INNER, z * INNER + (1 - y)

    barrier = pltpu.get_barrier_semaphore()
    for step in range(1, n_seq):
        pl.semaphore_signal(barrier, inc=1, device_id=dev(dp, (me + step) % n_seq), device_id_type=MESH)
    pl.semaphore_signal(barrier, inc=1, device_id=dev(across, me), device_id_type=MESH)

    @pl.when(has_left)
    def _():
        pl.semaphore_signal(barrier, inc=1, device_id=dev(left, me), device_id_type=MESH)

    @pl.when(has_right)
    def _():
        pl.semaphore_signal(barrier, inc=1, device_id=dev(right, me), device_id_type=MESH)

    pl.semaphore_wait(barrier, n_seq + has_left.astype(jnp.int32) + has_right.astype(jnp.int32))

    def piece_rows(piece):
        return pl.ds(piece * rows, rows)

    def h_copy(src, source, piece, send_sem, target):
        return pltpu.make_async_remote_copy(
            src_ref=src,
            dst_ref=hid.at[source, piece_rows(piece)],
            send_sem=send_sem,
            recv_sem=hr_sem.at[source, piece],
            device_id=dev(dp, target),
            device_id_type=MESH,
        )

    def h_to_x(step, piece):
        target = ((x + step) % n_x) * CORES + core
        return h_copy(h_ref.at[piece_rows(piece)], me, piece, hs_sem.at[step, piece], target)

    def h_to_mate(piece):
        return h_copy(h_ref.at[piece_rows(piece)], me, piece, hc_sem.at[piece], mate)

    def h_forward(step, piece):
        source = ((x + n_x - step) % n_x) * CORES + core
        return h_copy(hid.at[source, piece_rows(piece)], source, piece, hf_sem.at[step, piece], mate)

    def w_copy(shard, part, way, target, src=None):
        place = wbuf.at[own_rows(shard), pl.ds(part * LANES, LANES)]
        return pltpu.make_async_remote_copy(
            src_ref=place if src is None else src,
            dst_ref=place,
            send_sem=ws_sem.at[way, shard, part],
            recv_sem=wr_sem.at[shard, part],
            device_id=dev(target, me),
            device_id_type=MESH,
        )

    def w_own(part, way, target):
        return w_copy(dp, part, way, target, q_ref.at[:, q_cols] if part == 0 else None)

    def send_own(part, act):
        @pl.when(has_left)
        def _():
            act(w_own(part, 0, left))

        @pl.when(has_right)
        def _():
            act(w_own(part, 1, right))

        act(w_own(part, 2, across))

    start = lambda copy: copy.start()
    wait_send = lambda copy: copy.wait_send()

    for step in range(1, n_x):
        h_to_x(step, 0).start()
    send_own(0, start)
    for piece in range(1, PIECES):
        for step in range(1, n_x):
            h_to_x(step, piece).start()
    for piece in range(PIECES):
        h_to_mate(piece).start()

    local[0].wait()
    local[1].wait()
    lane_k = lax.broadcasted_iota(jnp.int32, (kd, LANES), 1)
    kw = kraw[...].astype(jnp.float32)
    vw = vraw[...].astype(jnp.float32)
    first = jnp.where(kv_odd, pltpu.roll(kw, HD, 1), kw)
    second = jnp.where(kv_odd, vw, pltpu.roll(vw, HD, 1))
    wbuf[own_rows(dp), LANES:] = jnp.where(lane_k < HD, first, second).astype(wbuf.dtype)
    local[2].wait()
    send_own(1, start)

    half = HD // 2
    ends = [len_ref[0, 0]]
    for j in range(1, docs):
        ends.append(ends[-1] + len_ref[0, j])
    lane = lax.broadcasted_iota(jnp.int32, (tok, LANES), 1)
    row = lax.broadcasted_iota(jnp.int32, (tok, LANES), 0)
    freqs = jnp.exp((lane % half).astype(jnp.float32) * (-2.0 / HD) * math.log(THETA))

    def key_range(block):
        low = max(0, block * tok - window)
        return low - low % tok, (block + 1) * tok

    def tables(block):
        pos = row + block * tok
        begin = jnp.zeros((tok, LANES), jnp.int32)
        for j in range(docs):
            begin = jnp.where(ends[j] <= pos, ends[j], begin)
        angle = (pos - begin).astype(jnp.float32) * freqs
        cos_buf[block * tok:(block + 1) * tok] = jnp.cos(angle)
        sine = jnp.sin(angle)
        sin_buf[block * tok:(block + 1) * tok] = jnp.where(lane % HD < half, -sine, sine)
        low, high = key_range(block)
        for number, base in enumerate(range(low, high, LANES)):
            key = lane + base
            fine = (key >= begin) & (key <= pos)
            bias[block, :, number * LANES:(number + 1) * LANES] = jnp.where(fine, 1.0, 0.0)

    def normalize(source, piece):
        floats = hid[source, piece_rows(piece)].astype(jnp.float32)
        scale = lax.rsqrt(jnp.mean(floats * floats, axis=-1, keepdims=True) + EPSILON)
        place = pl.ds(pl.multiple_of(source * tok, tok) + piece * rows, rows)
        nrm[place] = (floats * scale).astype(nrm.dtype)

    def relay_h(piece):
        for step in range(1, n_x):
            copy = h_forward(step, piece)
            copy.wait_recv()
            copy.start()
        for step in range(1, n_x):
            normalize(((x + n_x - step) % n_x) * CORES + core, piece)

    def relay_w(d):
        for part in range(2):
            @pl.when(z >= d)
            def _():
                shard = dp - d * INNER
                w_copy(shard, part, 1, dp).wait_recv()

                @pl.when(has_right)
                def _():
                    w_copy(shard, part, 1, right).start()

                w_copy(shard, part, 2, across).start()

            @pl.when(z + d < n_z)
            def _():
                shard = dp + d * INNER
                w_copy(shard, part, 0, dp).wait_recv()

                @pl.when(has_left)
                def _():
                    w_copy(shard, part, 0, left).start()

                w_copy(shard, part, 2, across).start()

    def mate_h(source, piece):
        h_copy(hid.at[source, piece_rows(piece)], source, piece, hc_sem.at[piece], mate).wait_recv()
        normalize(source, piece)

    local[3].wait()
    for piece in range(PIECES):
        normalize(me, piece)
    for piece in range(PIECES):
        mate_h(mate, piece)

    n_table = 0
    for turn in range(max(PIECES, n_z - 1)):
        if n_table < n_seq:
            tables(n_table)
            n_table += 1
        if turn < PIECES:
            relay_h(turn)
        if turn + 1 < n_z:
            relay_w(turn + 1)
    for block in range(n_table, n_seq):
        tables(block)

    for outer in range(n_z):
        shard = outer * INNER + (1 - y)
        for part in range(2):
            w_copy(shard, part, 2, across).wait_recv()
    for piece in range(PIECES):
        for step in range(1, n_x):
            mate_h(((x + n_x - step) % n_x) * CORES + (1 - core), piece)

    strip = math.gcd(length, 512)
    lane_s = lax.broadcasted_iota(jnp.int32, (strip, LANES), 1)
    low_half = lane_s % HD < half
    low_head = lane_s < HD
    for base in range(0, length, strip):
        place = slice(base, base + strip)
        lin = jnp.dot(nrm[place], wbuf[...], preferred_element_type=jnp.float32)
        cosine, sine = cos_buf[place], sin_buf[place]

        def rotate(part):
            other = jnp.where(low_half, pltpu.roll(part, LANES - half, 1), pltpu.roll(part, half, 1))
            return part * cosine + other * sine

        query, kv = lin[:, :LANES], lin[:, LANES:]
        query = rotate(query) * HD ** -0.5
        qs[0, place] = jnp.where(low_head, query, 0.0).astype(qs.dtype)
        qs[1, place] = jnp.where(low_head, 0.0, query).astype(qs.dtype)
        key = rotate(kv)
        ks[place] = jnp.where(low_head, key, pltpu.roll(key, HD, 1)).astype(ks.dtype)
        v0[place] = jnp.where(low_head, pltpu.roll(kv, HD, 1), 1.0).astype(v0.dtype)
        v1[place] = jnp.where(low_head, 1.0, kv).astype(v1.dtype)

    def o_copy(block):
        return pltpu.make_async_remote_copy(
            src_ref=ctx.at[block],
            dst_ref=out_ref.at[:, q_cols],
            send_sem=os_sem.at[block],
            recv_sem=or_sem.at[me],
            device_id=dev(dp, block),
            device_id_type=MESH,
        )

    low_tok = lax.broadcasted_iota(jnp.int32, (tok, LANES), 1) < HD
    for block in reversed(range(n_seq)):
        low, high = key_range(block)
        place = slice(block * tok, (block + 1) * tok)
        allowed = bias[block, :, :high - low] > 0.5
        outs = []
        for head, values in ((0, v0), (1, v1)):
            scores = lax.dot_general(
                qs[head, place], ks[low:high], (((1,), (1,)), ((), ())),
                preferred_element_type=jnp.float32,
            )
            scores = jnp.where(allowed, scores, NEG_FILL)
            highest = jnp.max(scores, axis=-1, keepdims=True)
            expons = jnp.exp(scores - highest).astype(values.dtype)
            outs.append(jnp.dot(expons, values[low:high], preferred_element_type=jnp.float32))
        mixed = jnp.where(low_tok, outs[0], outs[1])
        totals = pltpu.roll(jnp.where(low_tok, outs[1], outs[0]), HD, 1)
        ctx[block] = (mixed / totals).astype(ctx.dtype)

        @pl.when(me != block)
        def _():
            o_copy(block).start()

        @pl.when(me == block)
        def _():
            out_ref[:, q_cols] = ctx[block]

    for step in range(1, n_seq):
        source = (me + step) % n_seq
        cols = pl.ds(pl.multiple_of(source * LANES, LANES), LANES)
        pltpu.make_async_remote_copy(
            src_ref=ctx.at[0], dst_ref=out_ref.at[:, cols], send_sem=os_sem.at[0],
            recv_sem=or_sem.at[source], device_id=dev(dp, source), device_id_type=MESH,
        ).wait_recv()

    for block in range(n_seq):
        @pl.when(me != block)
        def _():
            o_copy(block).wait_send()
    for piece in range(PIECES):
        h_to_mate(piece).wait_send()
        for step in range(1, n_x):
            h_to_x(step, piece).wait_send()
            h_forward(step, piece).wait_send()
    for part in range(2):
        send_own(part, wait_send)
        for d in range(1, n_z):
            @pl.when(z >= d)
            def _():
                @pl.when(has_right)
                def _():
                    w_copy(dp - d * INNER, part, 1, right).wait_send()

                w_copy(dp - d * INNER, part, 2, across).wait_send()

            @pl.when(z + d < n_z)
            def _():
                @pl.when(has_left)
                def _():
                    w_copy(dp + d * INNER, part, 0, left).wait_send()

                w_copy(dp + d * INNER, part, 2, across).wait_send()


def shards(hidden_states, query_weight, key_weight, value_weight, doc_lengths):
    n_dp, n_seq = lax.axis_size("dp"), lax.axis_size("seq")
    tok, depth = hidden_states.shape
    kd = query_weight.shape[0]
    length = tok * n_seq
    docs = doc_lengths.shape[1]
    span = min(length, length // 2 + tok)
    half_type, full = jnp.bfloat16, jnp.float32
    any_spec = pl.BlockSpec(memory_space=pl.ANY)
    dma = pltpu.SemaphoreType.DMA
    n_x = n_seq // CORES
    return pl.pallas_call(
        functools.partial(kernel, n_dp, n_seq, docs),
        out_shape=jax.ShapeDtypeStruct((tok, query_weight.shape[1]), half_type),
        in_specs=[any_spec] * 4 + [pl.BlockSpec(memory_space=pltpu.SMEM)],
        out_specs=pl.BlockSpec(memory_space=pltpu.VMEM),
        scratch_shapes=[
            pltpu.VMEM((n_seq, tok, depth), half_type),
            pltpu.VMEM((length, depth), half_type),
            pltpu.VMEM((depth, 2 * LANES), half_type),
            pltpu.VMEM((kd, LANES), half_type),
            pltpu.VMEM((kd, LANES), half_type),
            pltpu.VMEM((length, LANES), full),
            pltpu.VMEM((length, LANES), full),
            pltpu.VMEM((n_seq, tok, span), full),
            pltpu.VMEM((2, length, LANES), half_type),
            pltpu.VMEM((length, LANES), half_type),
            pltpu.VMEM((length, LANES), half_type),
            pltpu.VMEM((length, LANES), half_type),
            pltpu.VMEM((n_seq, tok, LANES), half_type),
            dma((4,)),
            dma((n_x, PIECES)),
            dma((n_x, PIECES)),
            dma((PIECES,)),
            dma((n_seq, PIECES)),
            dma((3, n_dp, 2)),
            dma((n_dp, 2)),
            dma((n_seq,)),
            dma((n_seq,)),
        ],
        compiler_params=pltpu.CompilerParams(collective_id=0, has_side_effects=True),
    )(hidden_states, query_weight, key_weight, value_weight, doc_lengths)


def solution(mesh):
    placed = (P(("dp", "seq"), None), P("dp", None), P("dp", None), P("dp", None), P("dp", None))
    return jax.shard_map(
        shards, mesh=mesh, in_specs=placed, out_specs=P(("dp", "seq"), None), check_vma=False
    )
```

```python
import functools
import math

import jax
import jax.numpy as jnp
from jax import lax
from jax.experimental import pallas as pl
from jax.experimental.pallas import tpu as pltpu
from jax.sharding import PartitionSpec as P

HD = 64
GROUP = 4
LANES = 128
INNER = 2
CORES = 2
PIECES = 4
EPSILON = 1e-05
THETA = 500000.0
NEG_FILL = -1e30
MESH = pl.DeviceIdType.MESH


def kernel(n_dp, n_seq, docs, h_ref, q_ref, k_ref, v_ref, len_ref, out_ref,
           lens, hid, nrm, wbuf, kraw, vraw, cos_buf, sin_buf, bias, qs, ks, v0, v1, ctx,
           loc_sem, hs_sem, hf_sem, hc_sem, hr_sem, ws_sem, wr_sem, os_sem, or_sem):
    dp = lax.axis_index("dp")
    me = lax.axis_index("seq")
    tok, depth = h_ref.shape
    kd = q_ref.shape[0]
    length = tok * n_seq
    n_z = n_dp // INNER
    n_x = n_seq // CORES
    z, y = dp // INNER, dp % INNER
    x, core = me // CORES, me % CORES
    mate = x * CORES + (1 - core)
    rows = tok // PIECES
    kv_head = (me * (LANES // HD)) // GROUP
    kv_block = pl.multiple_of((kv_head * HD // LANES) * LANES, LANES)
    kv_odd = (kv_head * HD // LANES) * LANES != kv_head * HD
    window = length // 2

    def dev(d, s):
        return {"dp": d, "seq": s}

    def own_rows(index):
        return pl.ds(pl.multiple_of(index * kd, kd), kd)

    q_cols = pl.ds(pl.multiple_of(me * LANES, LANES), LANES)
    local = [
        pltpu.make_async_copy(k_ref.at[:, pl.ds(kv_block, LANES)], kraw, loc_sem.at[0]),
        pltpu.make_async_copy(v_ref.at[:, pl.ds(kv_block, LANES)], vraw, loc_sem.at[1]),
        pltpu.make_async_copy(q_ref.at[:, q_cols], wbuf.at[own_rows(dp), pl.ds(0, LANES)], loc_sem.at[2]),
        pltpu.make_async_copy(h_ref, hid.at[me], loc_sem.at[3]),
        pltpu.make_async_copy(len_ref, lens, loc_sem.at[4]),
    ]
    for copy in local:
        copy.start()

    has_left, has_right = z > 0, z < n_z - 1
    left, right, across = dp - INNER, dp + INNER, z * INNER + (1 - y)

    barrier = pltpu.get_barrier_semaphore()
    for step in range(1, n_seq):
        pl.semaphore_signal(barrier, inc=1, device_id=dev(dp, (me + step) % n_seq), device_id_type=MESH)
    pl.semaphore_signal(barrier, inc=1, device_id=dev(across, me), device_id_type=MESH)

    @pl.when(has_left)
    def _():
        pl.semaphore_signal(barrier, inc=1, device_id=dev(left, me), device_id_type=MESH)

    @pl.when(has_right)
    def _():
        pl.semaphore_signal(barrier, inc=1, device_id=dev(right, me), device_id_type=MESH)

    pl.semaphore_wait(barrier, n_seq + has_left.astype(jnp.int32) + has_right.astype(jnp.int32))

    def piece_rows(piece):
        return pl.ds(piece * rows, rows)

    def h_copy(src, source, piece, send_sem, target):
        return pltpu.make_async_remote_copy(
            src_ref=src,
            dst_ref=hid.at[source, piece_rows(piece)],
            send_sem=send_sem,
            recv_sem=hr_sem.at[source, piece],
            device_id=dev(dp, target),
            device_id_type=MESH,
        )

    def h_to_x(step, piece):
        target = ((x + step) % n_x) * CORES + core
        return h_copy(h_ref.at[piece_rows(piece)], me, piece, hs_sem.at[step, piece], target)

    def h_to_mate(piece):
        return h_copy(h_ref.at[piece_rows(piece)], me, piece, hc_sem.at[piece], mate)

    def h_forward(step, piece):
        source = ((x + n_x - step) % n_x) * CORES + core
        return h_copy(hid.at[source, piece_rows(piece)], source, piece, hf_sem.at[step, piece], mate)

    def w_copy(shard, part, way, target, src=None):
        place = wbuf.at[own_rows(shard), pl.ds(part * LANES, LANES)]
        return pltpu.make_async_remote_copy(
            src_ref=place if src is None else src,
            dst_ref=place,
            send_sem=ws_sem.at[way, shard, part],
            recv_sem=wr_sem.at[shard, part],
            device_id=dev(target, me),
            device_id_type=MESH,
        )

    def w_own(part, way, target):
        return w_copy(dp, part, way, target, q_ref.at[:, q_cols] if part == 0 else None)

    def send_own(part, act):
        @pl.when(has_left)
        def _():
            act(w_own(part, 0, left))

        @pl.when(has_right)
        def _():
            act(w_own(part, 1, right))

        act(w_own(part, 2, across))

    start = lambda copy: copy.start()
    wait_send = lambda copy: copy.wait_send()

    for step in range(1, n_x):
        h_to_x(step, 0).start()
    send_own(0, start)
    for piece in range(1, PIECES):
        for step in range(1, n_x):
            h_to_x(step, piece).start()
    for piece in range(PIECES):
        h_to_mate(piece).start()

    local[0].wait()
    local[1].wait()
    lane_k = lax.broadcasted_iota(jnp.int32, (kd, LANES), 1)
    kw = kraw[...].astype(jnp.float32)
    vw = vraw[...].astype(jnp.float32)
    first = jnp.where(kv_odd, pltpu.roll(kw, HD, 1), kw)
    second = jnp.where(kv_odd, vw, pltpu.roll(vw, HD, 1))
    wbuf[own_rows(dp), LANES:] = jnp.where(lane_k < HD, first, second).astype(wbuf.dtype)
    local[2].wait()
    send_own(1, start)

    half = HD // 2
    local[4].wait()
    ends = [lens[0, 0]]
    for j in range(1, docs):
        ends.append(ends[-1] + lens[0, j])
    lane = lax.broadcasted_iota(jnp.int32, (tok, LANES), 1)
    row = lax.broadcasted_iota(jnp.int32, (tok, LANES), 0)
    freqs = jnp.exp((lane % half).astype(jnp.float32) * (-2.0 / HD) * math.log(THETA))

    def key_range(block):
        low = max(0, block * tok - window)
        return low - low % tok, (block + 1) * tok

    def tables(block):
        pos = row + block * tok
        begin = jnp.zeros((tok, LANES), jnp.int32)
        for j in range(docs):
            begin = jnp.where(ends[j] <= pos, ends[j], begin)
        angle = (pos - begin).astype(jnp.float32) * freqs
        cos_buf[block * tok:(block + 1) * tok] = jnp.cos(angle)
        sine = jnp.sin(angle)
        sin_buf[block * tok:(block + 1) * tok] = jnp.where(lane % HD < half, -sine, sine)
        low, high = key_range(block)
        for number, base in enumerate(range(low, high, LANES)):
            key = lane + base
            fine = (key >= begin) & (key <= pos)
            bias[block, :, number * LANES:(number + 1) * LANES] = jnp.where(fine, 1.0, 0.0)

    def normalize(source, piece):
        floats = hid[source, piece_rows(piece)].astype(jnp.float32)
        scale = lax.rsqrt(jnp.mean(floats * floats, axis=-1, keepdims=True) + EPSILON)
        place = pl.ds(pl.multiple_of(source * tok, tok) + piece * rows, rows)
        nrm[place] = (floats * scale).astype(nrm.dtype)

    def relay_h(piece):
        for step in range(1, n_x):
            copy = h_forward(step, piece)
            copy.wait_recv()
            copy.start()
        for step in range(1, n_x):
            normalize(((x + n_x - step) % n_x) * CORES + core, piece)

    def relay_w(d):
        for part in range(2):
            @pl.when(z >= d)
            def _():
                shard = dp - d * INNER
                w_copy(shard, part, 1, dp).wait_recv()

                @pl.when(has_right)
                def _():
                    w_copy(shard, part, 1, right).start()

                w_copy(shard, part, 2, across).start()

            @pl.when(z + d < n_z)
            def _():
                shard = dp + d * INNER
                w_copy(shard, part, 0, dp).wait_recv()

                @pl.when(has_left)
                def _():
                    w_copy(shard, part, 0, left).start()

                w_copy(shard, part, 2, across).start()

    def mate_h(source, piece):
        h_copy(hid.at[source, piece_rows(piece)], source, piece, hc_sem.at[piece], mate).wait_recv()
        normalize(source, piece)

    local[3].wait()
    for piece in range(PIECES):
        normalize(me, piece)
    for piece in range(PIECES):
        mate_h(mate, piece)

    def far_mate(piece):
        for step in range(1, n_x):
            mate_h(((x + n_x - step) % n_x) * CORES + (1 - core), piece)

    tables(0)
    n_table = 1
    turns = max(PIECES, n_z - 1)
    for turn in range(turns):
        if turn + 1 < n_z:
            relay_w(turn + 1)
        if turn < PIECES:
            relay_h(turn)
        if 0 < turn < PIECES:
            far_mate(turn - 1)
        if n_table < n_seq and turn + 1 < turns:
            tables(n_table)
            n_table += 1
    for block in range(n_table, n_seq):
        tables(block)

    for outer in range(n_z):
        shard = outer * INNER + (1 - y)
        for part in range(2):
            w_copy(shard, part, 2, across).wait_recv()
    far_mate(PIECES - 1)

    strip = math.gcd(length, 512)
    lane_s = lax.broadcasted_iota(jnp.int32, (strip, LANES), 1)
    low_half = lane_s % HD < half
    low_head = lane_s < HD
    for base in range(0, length, strip):
        place = slice(base, base + strip)
        lin = jnp.dot(nrm[place], wbuf[...], preferred_element_type=jnp.float32)
        cosine, sine = cos_buf[place], sin_buf[place]

        def rotate(part):
            other = jnp.where(low_half, pltpu.roll(part, LANES - half, 1), pltpu.roll(part, half, 1))
            return part * cosine + other * sine

        query, kv = lin[:, :LANES], lin[:, LANES:]
        query = rotate(query) * HD ** -0.5
        qs[0, place] = jnp.where(low_head, query, 0.0).astype(qs.dtype)
        qs[1, place] = jnp.where(low_head, 0.0, query).astype(qs.dtype)
        key = rotate(kv)
        ks[place] = jnp.where(low_head, key, pltpu.roll(key, HD, 1)).astype(ks.dtype)
        v0[place] = jnp.where(low_head, pltpu.roll(kv, HD, 1), 1.0).astype(v0.dtype)
        v1[place] = jnp.where(low_head, 1.0, kv).astype(v1.dtype)

    def o_copy(block):
        return pltpu.make_async_remote_copy(
            src_ref=ctx.at[block],
            dst_ref=out_ref.at[:, q_cols],
            send_sem=os_sem.at[block],
            recv_sem=or_sem.at[me],
            device_id=dev(dp, block),
            device_id_type=MESH,
        )

    low_tok = lax.broadcasted_iota(jnp.int32, (tok, LANES), 1) < HD
    for block in reversed(range(n_seq)):
        low, high = key_range(block)
        place = slice(block * tok, (block + 1) * tok)
        allowed = bias[block, :, :high - low] > 0.5
        outs = []
        for head, values in ((0, v0), (1, v1)):
            scores = lax.dot_general(
                qs[head, place], ks[low:high], (((1,), (1,)), ((), ())),
                preferred_element_type=jnp.float32,
            )
            scores = jnp.where(allowed, scores, NEG_FILL)
            highest = jnp.max(scores, axis=-1, keepdims=True)
            expons = jnp.exp(scores - highest).astype(values.dtype)
            outs.append(jnp.dot(expons, values[low:high], preferred_element_type=jnp.float32))
        mixed = jnp.where(low_tok, outs[0], outs[1])
        totals = pltpu.roll(jnp.where(low_tok, outs[1], outs[0]), HD, 1)
        ctx[block] = (mixed / totals).astype(ctx.dtype)

        @pl.when(me != block)
        def _():
            o_copy(block).start()

        @pl.when(me == block)
        def _():
            out_ref[:, q_cols] = ctx[block]

    for step in range(1, n_seq):
        source = (me + step) % n_seq
        cols = pl.ds(pl.multiple_of(source * LANES, LANES), LANES)
        pltpu.make_async_remote_copy(
            src_ref=ctx.at[0], dst_ref=out_ref.at[:, cols], send_sem=os_sem.at[0],
            recv_sem=or_sem.at[source], device_id=dev(dp, source), device_id_type=MESH,
        ).wait_recv()

    for block in range(n_seq):
        @pl.when(me != block)
        def _():
            o_copy(block).wait_send()
    for piece in range(PIECES):
        h_to_mate(piece).wait_send()
        for step in range(1, n_x):
            h_to_x(step, piece).wait_send()
            h_forward(step, piece).wait_send()
    for part in range(2):
        send_own(part, wait_send)
        for d in range(1, n_z):
            @pl.when(z >= d)
            def _():
                @pl.when(has_right)
                def _():
                    w_copy(dp - d * INNER, part, 1, right).wait_send()

                w_copy(dp - d * INNER, part, 2, across).wait_send()

            @pl.when(z + d < n_z)
            def _():
                @pl.when(has_left)
                def _():
                    w_copy(dp + d * INNER, part, 0, left).wait_send()

                w_copy(dp + d * INNER, part, 2, across).wait_send()


def shards(hidden_states, query_weight, key_weight, value_weight, doc_lengths):
    n_dp, n_seq = lax.axis_size("dp"), lax.axis_size("seq")
    tok, depth = hidden_states.shape
    kd = query_weight.shape[0]
    length = tok * n_seq
    docs = doc_lengths.shape[1]
    span = min(length, length // 2 + tok)
    half_type, full = jnp.bfloat16, jnp.float32
    any_spec = pl.BlockSpec(memory_space=pl.ANY)
    dma = pltpu.SemaphoreType.DMA
    n_x = n_seq // CORES
    return pl.pallas_call(
        functools.partial(kernel, n_dp, n_seq, docs),
        out_shape=pltpu.VMEM((tok, query_weight.shape[1]), half_type),
        in_specs=[any_spec] * 5,
        out_specs=pl.BlockSpec(memory_space=pltpu.VMEM),
        scratch_shapes=[
            pltpu.SMEM((1, docs), jnp.int32),
            pltpu.VMEM((n_seq, tok, depth), half_type),
            pltpu.VMEM((length, depth), half_type),
            pltpu.VMEM((depth, 2 * LANES), half_type),
            pltpu.VMEM((kd, LANES), half_type),
            pltpu.VMEM((kd, LANES), half_type),
            pltpu.VMEM((length, LANES), full),
            pltpu.VMEM((length, LANES), full),
            pltpu.VMEM((n_seq, tok, span), full),
            pltpu.VMEM((2, length, LANES), half_type),
            pltpu.VMEM((length, LANES), half_type),
            pltpu.VMEM((length, LANES), half_type),
            pltpu.VMEM((length, LANES), half_type),
            pltpu.VMEM((n_seq, tok, LANES), half_type),
            dma((5,)),
            dma((n_x, PIECES)),
            dma((n_x, PIECES)),
            dma((PIECES,)),
            dma((n_seq, PIECES)),
            dma((3, n_dp, 2)),
            dma((n_dp, 2)),
            dma((n_seq,)),
            dma((n_seq,)),
        ],
        compiler_params=pltpu.CompilerParams(collective_id=0, has_side_effects=True),
    )(hidden_states, query_weight, key_weight, value_weight, doc_lengths)


def solution(mesh):
    placed = (P(("dp", "seq"), None), P("dp", None), P("dp", None), P("dp", None), P("dp", None))
    return jax.shard_map(
        shards, mesh=mesh, in_specs=placed, out_specs=P(("dp", "seq"), None), check_vma=False
    )
```

```python
import functools
import math

import jax
import jax.numpy as jnp
from jax import lax
from jax.experimental import pallas as pl
from jax.experimental.pallas import tpu as pltpu
from jax.sharding import PartitionSpec as P

HD = 64
GROUP = 4
LANES = 128
INNER = 2
CORES = 2
PIECES = 8
EPSILON = 1e-05
THETA = 500000.0
NEG_FILL = -1e30
MESH = pl.DeviceIdType.MESH


def kernel(n_dp, n_seq, docs, h_ref, q_ref, k_ref, v_ref, len_ref, out_ref,
           lens, hid, nrm, wbuf, kraw, vraw, cos_buf, sin_buf, bias, qs, ks, v0, v1, ctx,
           loc_sem, hs_sem, hf_sem, hc_sem, hr_sem, ws_sem, wr_sem, os_sem, or_sem):
    dp = lax.axis_index("dp")
    me = lax.axis_index("seq")
    tok, depth = h_ref.shape
    kd = q_ref.shape[0]
    length = tok * n_seq
    n_z = n_dp // INNER
    n_x = n_seq // CORES
    z, y = dp // INNER, dp % INNER
    x, core = me // CORES, me % CORES
    mate = x * CORES + (1 - core)
    rows = tok // PIECES
    kv_head = (me * (LANES // HD)) // GROUP
    kv_block = pl.multiple_of((kv_head * HD // LANES) * LANES, LANES)
    kv_odd = (kv_head * HD // LANES) * LANES != kv_head * HD
    window = length // 2

    def dev(d, s):
        return {"dp": d, "seq": s}

    def own_rows(index):
        return pl.ds(pl.multiple_of(index * kd, kd), kd)

    q_cols = pl.ds(pl.multiple_of(me * LANES, LANES), LANES)
    local = [
        pltpu.make_async_copy(k_ref.at[:, pl.ds(kv_block, LANES)], kraw, loc_sem.at[0]),
        pltpu.make_async_copy(v_ref.at[:, pl.ds(kv_block, LANES)], vraw, loc_sem.at[1]),
        pltpu.make_async_copy(q_ref.at[:, q_cols], wbuf.at[own_rows(dp), pl.ds(0, LANES)], loc_sem.at[2]),
        pltpu.make_async_copy(h_ref, hid.at[me], loc_sem.at[3]),
        pltpu.make_async_copy(len_ref, lens, loc_sem.at[4]),
    ]
    for copy in local:
        copy.start()

    has_left, has_right = z > 0, z < n_z - 1
    left, right, across = dp - INNER, dp + INNER, z * INNER + (1 - y)

    barrier = pltpu.get_barrier_semaphore()
    for step in range(1, n_seq):
        pl.semaphore_signal(barrier, inc=1, device_id=dev(dp, (me + step) % n_seq), device_id_type=MESH)
    pl.semaphore_signal(barrier, inc=1, device_id=dev(across, me), device_id_type=MESH)

    @pl.when(has_left)
    def _():
        pl.semaphore_signal(barrier, inc=1, device_id=dev(left, me), device_id_type=MESH)

    @pl.when(has_right)
    def _():
        pl.semaphore_signal(barrier, inc=1, device_id=dev(right, me), device_id_type=MESH)

    pl.semaphore_wait(barrier, n_seq + has_left.astype(jnp.int32) + has_right.astype(jnp.int32))

    def piece_rows(piece):
        return pl.ds(piece * rows, rows)

    def h_copy(src, source, piece, send_sem, target):
        return pltpu.make_async_remote_copy(
            src_ref=src,
            dst_ref=hid.at[source, piece_rows(piece)],
            send_sem=send_sem,
            recv_sem=hr_sem.at[source, piece],
            device_id=dev(dp, target),
            device_id_type=MESH,
        )

    def h_to_x(step, piece):
        target = ((x + step) % n_x) * CORES + core
        return h_copy(h_ref.at[piece_rows(piece)], me, piece, hs_sem.at[step, piece], target)

    def h_to_mate(piece):
        return h_copy(h_ref.at[piece_rows(piece)], me, piece, hc_sem.at[piece], mate)

    def h_forward(step, piece):
        source = ((x + n_x - step) % n_x) * CORES + core
        return h_copy(hid.at[source, piece_rows(piece)], source, piece, hf_sem.at[step, piece], mate)

    def w_copy(shard, part, way, target, src=None):
        place = wbuf.at[own_rows(shard), pl.ds(part * LANES, LANES)]
        return pltpu.make_async_remote_copy(
            src_ref=place if src is None else src,
            dst_ref=place,
            send_sem=ws_sem.at[way, shard, part],
            recv_sem=wr_sem.at[shard, part],
            device_id=dev(target, me),
            device_id_type=MESH,
        )

    def w_own(part, way, target):
        return w_copy(dp, part, way, target, q_ref.at[:, q_cols] if part == 0 else None)

    def send_own(part, act):
        @pl.when(has_left)
        def _():
            act(w_own(part, 0, left))

        @pl.when(has_right)
        def _():
            act(w_own(part, 1, right))

        act(w_own(part, 2, across))

    start = lambda copy: copy.start()
    wait_send = lambda copy: copy.wait_send()

    for step in range(1, n_x):
        h_to_x(step, 0).start()
    send_own(0, start)
    for piece in range(1, PIECES):
        for step in range(1, n_x):
            h_to_x(step, piece).start()
    for piece in range(PIECES):
        h_to_mate(piece).start()

    local[0].wait()
    local[1].wait()
    lane_k = lax.broadcasted_iota(jnp.int32, (kd, LANES), 1)
    kw = kraw[...].astype(jnp.float32)
    vw = vraw[...].astype(jnp.float32)
    first = jnp.where(kv_odd, pltpu.roll(kw, HD, 1), kw)
    second = jnp.where(kv_odd, vw, pltpu.roll(vw, HD, 1))
    wbuf[own_rows(dp), LANES:] = jnp.where(lane_k < HD, first, second).astype(wbuf.dtype)
    local[2].wait()
    send_own(1, start)

    half = HD // 2
    local[4].wait()
    ends = [lens[0, 0]]
    for j in range(1, docs):
        ends.append(ends[-1] + lens[0, j])
    lane = lax.broadcasted_iota(jnp.int32, (tok, LANES), 1)
    row = lax.broadcasted_iota(jnp.int32, (tok, LANES), 0)
    freqs = jnp.exp((lane % half).astype(jnp.float32) * (-2.0 / HD) * math.log(THETA))

    def key_range(block):
        low = max(0, block * tok - window)
        return low - low % tok, (block + 1) * tok

    def tables(block):
        pos = row + block * tok
        begin = jnp.zeros((tok, LANES), jnp.int32)
        for j in range(docs):
            begin = jnp.where(ends[j] <= pos, ends[j], begin)
        angle = (pos - begin).astype(jnp.float32) * freqs
        cos_buf[block * tok:(block + 1) * tok] = jnp.cos(angle)
        sine = jnp.sin(angle)
        sin_buf[block * tok:(block + 1) * tok] = jnp.where(lane % HD < half, -sine, sine)
        low, high = key_range(block)
        for number, base in enumerate(range(low, high, LANES)):
            key = lane + base
            fine = (key >= begin) & (key <= pos)
            bias[block, :, number * LANES:(number + 1) * LANES] = jnp.where(fine, 1.0, 0.0)

    def normalize(source, piece):
        floats = hid[source, piece_rows(piece)].astype(jnp.float32)
        scale = lax.rsqrt(jnp.mean(floats * floats, axis=-1, keepdims=True) + EPSILON)
        place = pl.ds(pl.multiple_of(source * tok, tok) + piece * rows, rows)
        nrm[place] = (floats * scale).astype(nrm.dtype)

    def relay_h(piece):
        for step in range(1, n_x):
            copy = h_forward(step, piece)
            copy.wait_recv()
            copy.start()
        for step in range(1, n_x):
            normalize(((x + n_x - step) % n_x) * CORES + core, piece)

    def relay_w(d):
        for part in range(2):
            @pl.when(z >= d)
            def _():
                shard = dp - d * INNER
                w_copy(shard, part, 1, dp).wait_recv()

                @pl.when(has_right)
                def _():
                    w_copy(shard, part, 1, right).start()

                w_copy(shard, part, 2, across).start()

            @pl.when(z + d < n_z)
            def _():
                shard = dp + d * INNER
                w_copy(shard, part, 0, dp).wait_recv()

                @pl.when(has_left)
                def _():
                    w_copy(shard, part, 0, left).start()

                w_copy(shard, part, 2, across).start()

    def mate_h(source, piece):
        h_copy(hid.at[source, piece_rows(piece)], source, piece, hc_sem.at[piece], mate).wait_recv()
        normalize(source, piece)

    local[3].wait()
    for piece in range(PIECES):
        normalize(me, piece)
    for piece in range(PIECES):
        mate_h(mate, piece)

    def far_mate(piece):
        for step in range(1, n_x):
            mate_h(((x + n_x - step) % n_x) * CORES + (1 - core), piece)

    tables(0)
    n_table = 1
    stride = max(1, PIECES // 4)
    turns = max(PIECES, stride * (n_z - 1))
    for turn in range(turns):
        if turn % stride == 0 and turn // stride + 1 < n_z:
            relay_w(turn // stride + 1)
        if turn < PIECES:
            relay_h(turn)
        if 0 < turn < PIECES:
            far_mate(turn - 1)
        if n_table < n_seq and turn + 1 < turns:
            tables(n_table)
            n_table += 1
    for block in range(n_table, n_seq):
        tables(block)

    for outer in range(n_z):
        shard = outer * INNER + (1 - y)
        for part in range(2):
            w_copy(shard, part, 2, across).wait_recv()

    strip = CORES * tok
    lane_s = lax.broadcasted_iota(jnp.int32, (strip, LANES), 1)
    low_half = lane_s % HD < half
    low_head = lane_s < HD
    for step in range(n_x):
        if step == 1:
            far_mate(PIECES - 1)
        place = pl.ds(pl.multiple_of(((x + n_x - step) % n_x) * strip, strip), strip)
        lin = jnp.dot(nrm[place], wbuf[...], preferred_element_type=jnp.float32)
        cosine, sine = cos_buf[place], sin_buf[place]

        def rotate(part):
            other = jnp.where(low_half, pltpu.roll(part, LANES - half, 1), pltpu.roll(part, half, 1))
            return part * cosine + other * sine

        query, kv = lin[:, :LANES], lin[:, LANES:]
        query = rotate(query) * HD ** -0.5
        qs[0, place] = jnp.where(low_head, query, 0.0).astype(qs.dtype)
        qs[1, place] = jnp.where(low_head, 0.0, query).astype(qs.dtype)
        key = rotate(kv)
        ks[place] = jnp.where(low_head, key, pltpu.roll(key, HD, 1)).astype(ks.dtype)
        v0[place] = jnp.where(low_head, pltpu.roll(kv, HD, 1), 1.0).astype(v0.dtype)
        v1[place] = jnp.where(low_head, 1.0, kv).astype(v1.dtype)

    def o_copy(block):
        return pltpu.make_async_remote_copy(
            src_ref=ctx.at[block],
            dst_ref=out_ref.at[:, q_cols],
            send_sem=os_sem.at[block],
            recv_sem=or_sem.at[me],
            device_id=dev(dp, block),
            device_id_type=MESH,
        )

    low_tok = lax.broadcasted_iota(jnp.int32, (tok, LANES), 1) < HD
    for block in reversed(range(n_seq)):
        low, high = key_range(block)
        place = slice(block * tok, (block + 1) * tok)
        allowed = bias[block, :, :high - low] > 0.5
        outs = []
        for head, values in ((0, v0), (1, v1)):
            scores = lax.dot_general(
                qs[head, place], ks[low:high], (((1,), (1,)), ((), ())),
                preferred_element_type=jnp.float32,
            )
            scores = jnp.where(allowed, scores, NEG_FILL)
            highest = jnp.max(scores, axis=-1, keepdims=True)
            expons = jnp.exp(scores - highest).astype(values.dtype)
            outs.append(jnp.dot(expons, values[low:high], preferred_element_type=jnp.float32))
        mixed = jnp.where(low_tok, outs[0], outs[1])
        totals = pltpu.roll(jnp.where(low_tok, outs[1], outs[0]), HD, 1)
        ctx[block] = (mixed / totals).astype(ctx.dtype)

        @pl.when(me != block)
        def _():
            o_copy(block).start()

        @pl.when(me == block)
        def _():
            out_ref[:, q_cols] = ctx[block]

    for step in range(1, n_seq):
        source = (me + step) % n_seq
        cols = pl.ds(pl.multiple_of(source * LANES, LANES), LANES)
        pltpu.make_async_remote_copy(
            src_ref=ctx.at[0], dst_ref=out_ref.at[:, cols], send_sem=os_sem.at[0],
            recv_sem=or_sem.at[source], device_id=dev(dp, source), device_id_type=MESH,
        ).wait_recv()

    for block in range(n_seq):
        @pl.when(me != block)
        def _():
            o_copy(block).wait_send()
    for piece in range(PIECES):
        h_to_mate(piece).wait_send()
        for step in range(1, n_x):
            h_to_x(step, piece).wait_send()
            h_forward(step, piece).wait_send()
    for part in range(2):
        send_own(part, wait_send)
        for d in range(1, n_z):
            @pl.when(z >= d)
            def _():
                @pl.when(has_right)
                def _():
                    w_copy(dp - d * INNER, part, 1, right).wait_send()

                w_copy(dp - d * INNER, part, 2, across).wait_send()

            @pl.when(z + d < n_z)
            def _():
                @pl.when(has_left)
                def _():
                    w_copy(dp + d * INNER, part, 0, left).wait_send()

                w_copy(dp + d * INNER, part, 2, across).wait_send()


def shards(hidden_states, query_weight, key_weight, value_weight, doc_lengths):
    n_dp, n_seq = lax.axis_size("dp"), lax.axis_size("seq")
    tok, depth = hidden_states.shape
    kd = query_weight.shape[0]
    length = tok * n_seq
    docs = doc_lengths.shape[1]
    span = min(length, length // 2 + tok)
    half_type, full = jnp.bfloat16, jnp.float32
    any_spec = pl.BlockSpec(memory_space=pl.ANY)
    dma = pltpu.SemaphoreType.DMA
    n_x = n_seq // CORES
    return pl.pallas_call(
        functools.partial(kernel, n_dp, n_seq, docs),
        out_shape=pltpu.VMEM((tok, query_weight.shape[1]), half_type),
        in_specs=[any_spec] * 5,
        out_specs=pl.BlockSpec(memory_space=pltpu.VMEM),
        scratch_shapes=[
            pltpu.SMEM((1, docs), jnp.int32),
            pltpu.VMEM((n_seq, tok, depth), half_type),
            pltpu.VMEM((length, depth), half_type),
            pltpu.VMEM((depth, 2 * LANES), half_type),
            pltpu.VMEM((kd, LANES), half_type),
            pltpu.VMEM((kd, LANES), half_type),
            pltpu.VMEM((length, LANES), full),
            pltpu.VMEM((length, LANES), full),
            pltpu.VMEM((n_seq, tok, span), full),
            pltpu.VMEM((2, length, LANES), half_type),
            pltpu.VMEM((length, LANES), half_type),
            pltpu.VMEM((length, LANES), half_type),
            pltpu.VMEM((length, LANES), half_type),
            pltpu.VMEM((n_seq, tok, LANES), half_type),
            dma((5,)),
            dma((n_x, PIECES)),
            dma((n_x, PIECES)),
            dma((PIECES,)),
            dma((n_seq, PIECES)),
            dma((3, n_dp, 2)),
            dma((n_dp, 2)),
            dma((n_seq,)),
            dma((n_seq,)),
        ],
        compiler_params=pltpu.CompilerParams(collective_id=0, has_side_effects=True),
    )(hidden_states, query_weight, key_weight, value_weight, doc_lengths)


def solution(mesh):
    placed = (P(("dp", "seq"), None), P("dp", None), P("dp", None), P("dp", None), P("dp", None))
    return jax.shard_map(
        shards, mesh=mesh, in_specs=placed, out_specs=P(("dp", "seq"), None), check_vma=False
    )
```

```python
import functools
import math

import jax
import jax.numpy as jnp
from jax import lax
from jax.experimental import pallas as pl
from jax.experimental.pallas import tpu as pltpu
from jax.sharding import PartitionSpec as P

HD = 64
GROUP = 4
LANES = 128
INNER = 2
CORES = 2
PIECES = 4
PARTS = 4
EPSILON = 1e-05
THETA = 500000.0
NEG_FILL = -1e30
MESH = pl.DeviceIdType.MESH


def kernel(n_dp, n_seq, docs, h_ref, q_ref, k_ref, v_ref, len_ref, out_ref,
           lens, hid, nrm, wbuf, kraw, vraw, cos_buf, sin_buf, bias, qs, ks, v0, v1, ctx,
           loc_sem, hs_sem, hf_sem, hc_sem, hr_sem, ws_sem, wr_sem, os_sem, or_sem):
    dp = lax.axis_index("dp")
    me = lax.axis_index("seq")
    tok, depth = h_ref.shape
    kd = q_ref.shape[0]
    length = tok * n_seq
    n_z = n_dp // INNER
    n_x = n_seq // CORES
    z, y = dp // INNER, dp % INNER
    x, core = me // CORES, me % CORES
    mate = x * CORES + (1 - core)
    rows = tok // PIECES
    kv_head = (me * (LANES // HD)) // GROUP
    kv_block = pl.multiple_of((kv_head * HD // LANES) * LANES, LANES)
    kv_odd = (kv_head * HD // LANES) * LANES != kv_head * HD
    window = length // 2

    def dev(d, s):
        return {"dp": d, "seq": s}

    def own_rows(index):
        return pl.ds(pl.multiple_of(index * kd, kd), kd)

    q_cols = pl.ds(pl.multiple_of(me * LANES, LANES), LANES)
    local = [
        pltpu.make_async_copy(k_ref.at[:, pl.ds(kv_block, LANES)], kraw, loc_sem.at[0]),
        pltpu.make_async_copy(v_ref.at[:, pl.ds(kv_block, LANES)], vraw, loc_sem.at[1]),
        pltpu.make_async_copy(q_ref.at[:, q_cols], wbuf.at[own_rows(dp), pl.ds(0, LANES)], loc_sem.at[2]),
        pltpu.make_async_copy(h_ref, hid.at[me], loc_sem.at[3]),
        pltpu.make_async_copy(len_ref, lens, loc_sem.at[4]),
    ]
    for copy in local:
        copy.start()

    has_left, has_right = z > 0, z < n_z - 1
    left, right, across = dp - INNER, dp + INNER, z * INNER + (1 - y)

    barrier = pltpu.get_barrier_semaphore()
    for step in range(1, n_seq):
        pl.semaphore_signal(barrier, inc=1, device_id=dev(dp, (me + step) % n_seq), device_id_type=MESH)
    pl.semaphore_signal(barrier, inc=1, device_id=dev(across, me), device_id_type=MESH)

    @pl.when(has_left)
    def _():
        pl.semaphore_signal(barrier, inc=1, device_id=dev(left, me), device_id_type=MESH)

    @pl.when(has_right)
    def _():
        pl.semaphore_signal(barrier, inc=1, device_id=dev(right, me), device_id_type=MESH)

    pl.semaphore_wait(barrier, n_seq + has_left.astype(jnp.int32) + has_right.astype(jnp.int32))

    def piece_rows(piece):
        return pl.ds(piece * rows, rows)

    def h_copy(src, source, piece, send_sem, target):
        return pltpu.make_async_remote_copy(
            src_ref=src,
            dst_ref=hid.at[source, piece_rows(piece)],
            send_sem=send_sem,
            recv_sem=hr_sem.at[source, piece],
            device_id=dev(dp, target),
            device_id_type=MESH,
        )

    def h_to_x(step, piece):
        target = ((x + step) % n_x) * CORES + core
        return h_copy(h_ref.at[piece_rows(piece)], me, piece, hs_sem.at[step, piece], target)

    def h_to_mate(piece):
        return h_copy(h_ref.at[piece_rows(piece)], me, piece, hc_sem.at[piece], mate)

    def h_forward(step, piece):
        source = ((x + n_x - step) % n_x) * CORES + core
        return h_copy(hid.at[source, piece_rows(piece)], source, piece, hf_sem.at[step, piece], mate)

    def w_copy(shard, part, way, target, src=None):
        base = pl.multiple_of(shard * kd + (part % 2) * (kd // 2), kd // 2)
        place = wbuf.at[pl.ds(base, kd // 2), pl.ds(part // 2 * LANES, LANES)]
        return pltpu.make_async_remote_copy(
            src_ref=place if src is None else src,
            dst_ref=place,
            send_sem=ws_sem.at[way, shard, part],
            recv_sem=wr_sem.at[shard, part],
            device_id=dev(target, me),
            device_id_type=MESH,
        )

    def w_own(part, way, target):
        src = q_ref.at[pl.ds((part % 2) * (kd // 2), kd // 2), q_cols] if part < 2 else None
        return w_copy(dp, part, way, target, src)

    def send_own(part, act):
        @pl.when(has_left)
        def _():
            act(w_own(part, 0, left))

        @pl.when(has_right)
        def _():
            act(w_own(part, 1, right))

        act(w_own(part, 2, across))

    start = lambda copy: copy.start()
    wait_send = lambda copy: copy.wait_send()

    for step in range(1, n_x):
        h_to_x(step, 0).start()
    send_own(0, start)
    send_own(1, start)
    for piece in range(1, PIECES):
        for step in range(1, n_x):
            h_to_x(step, piece).start()
    for piece in range(PIECES):
        h_to_mate(piece).start()

    local[0].wait()
    local[1].wait()
    lane_k = lax.broadcasted_iota(jnp.int32, (kd, LANES), 1)
    kw = kraw[...].astype(jnp.float32)
    vw = vraw[...].astype(jnp.float32)
    first = jnp.where(kv_odd, pltpu.roll(kw, HD, 1), kw)
    second = jnp.where(kv_odd, vw, pltpu.roll(vw, HD, 1))
    wbuf[own_rows(dp), LANES:] = jnp.where(lane_k < HD, first, second).astype(wbuf.dtype)
    local[2].wait()
    send_own(2, start)
    send_own(3, start)

    half = HD // 2
    local[4].wait()
    ends = [lens[0, 0]]
    for j in range(1, docs):
        ends.append(ends[-1] + lens[0, j])
    lane = lax.broadcasted_iota(jnp.int32, (tok, LANES), 1)
    row = lax.broadcasted_iota(jnp.int32, (tok, LANES), 0)
    freqs = jnp.exp((lane % half).astype(jnp.float32) * (-2.0 / HD) * math.log(THETA))

    def key_range(block):
        low = max(0, block * tok - window)
        return low - low % tok, (block + 1) * tok

    def tables(block):
        pos = row + block * tok
        begin = jnp.zeros((tok, LANES), jnp.int32)
        for j in range(docs):
            begin = jnp.where(ends[j] <= pos, ends[j], begin)
        angle = (pos - begin).astype(jnp.float32) * freqs
        cos_buf[block * tok:(block + 1) * tok] = jnp.cos(angle)
        sine = jnp.sin(angle)
        sin_buf[block * tok:(block + 1) * tok] = jnp.where(lane % HD < half, -sine, sine)
        low, high = key_range(block)
        for number, base in enumerate(range(low, high, LANES)):
            key = lane + base
            fine = (key >= begin) & (key <= pos)
            bias[block, :, number * LANES:(number + 1) * LANES] = jnp.where(fine, 1.0, 0.0)

    def normalize(source, piece):
        floats = hid[source, piece_rows(piece)].astype(jnp.float32)
        scale = lax.rsqrt(jnp.mean(floats * floats, axis=-1, keepdims=True) + EPSILON)
        place = pl.ds(pl.multiple_of(source * tok, tok) + piece * rows, rows)
        nrm[place] = (floats * scale).astype(nrm.dtype)

    def relay_h(piece):
        for step in range(1, n_x):
            copy = h_forward(step, piece)
            copy.wait_recv()
            copy.start()
        for step in range(1, n_x):
            normalize(((x + n_x - step) % n_x) * CORES + core, piece)

    def relay_w(d):
        for part in range(PARTS):
            @pl.when(z >= d)
            def _():
                shard = dp - d * INNER
                w_copy(shard, part, 1, dp).wait_recv()

                @pl.when(has_right)
                def _():
                    w_copy(shard, part, 1, right).start()

                w_copy(shard, part, 2, across).start()

            @pl.when(z + d < n_z)
            def _():
                shard = dp + d * INNER
                w_copy(shard, part, 0, dp).wait_recv()

                @pl.when(has_left)
                def _():
                    w_copy(shard, part, 0, left).start()

                w_copy(shard, part, 2, across).start()

    def mate_h(source, piece):
        h_copy(hid.at[source, piece_rows(piece)], source, piece, hc_sem.at[piece], mate).wait_recv()
        normalize(source, piece)

    local[3].wait()
    for piece in range(PIECES):
        normalize(me, piece)
    for piece in range(PIECES):
        mate_h(mate, piece)

    def far_mate(piece):
        for step in range(1, n_x):
            mate_h(((x + n_x - step) % n_x) * CORES + (1 - core), piece)

    tables(0)
    n_table = 1
    turns = max(PIECES, n_z - 1)
    for turn in range(turns):
        if turn + 1 < n_z:
            relay_w(turn + 1)
        if turn < PIECES:
            relay_h(turn)
        if 0 < turn < PIECES:
            far_mate(turn - 1)
        if n_table < n_seq and turn + 1 < turns:
            tables(n_table)
            n_table += 1
    for block in range(n_table, n_seq):
        tables(block)

    for outer in range(n_z):
        shard = outer * INNER + (1 - y)
        for part in range(PARTS):
            w_copy(shard, part, 2, across).wait_recv()
    far_mate(PIECES - 1)

    strip = math.gcd(length, 512)
    lane_s = lax.broadcasted_iota(jnp.int32, (strip, LANES), 1)
    low_half = lane_s % HD < half
    low_head = lane_s < HD
    for base in range(0, length, strip):
        place = slice(base, base + strip)
        lin = jnp.dot(nrm[place], wbuf[...], preferred_element_type=jnp.float32)
        cosine, sine = cos_buf[place], sin_buf[place]

        def rotate(part):
            other = jnp.where(low_half, pltpu.roll(part, LANES - half, 1), pltpu.roll(part, half, 1))
            return part * cosine + other * sine

        query, kv = lin[:, :LANES], lin[:, LANES:]
        query = rotate(query) * HD ** -0.5
        qs[0, place] = jnp.where(low_head, query, 0.0).astype(qs.dtype)
        qs[1, place] = jnp.where(low_head, 0.0, query).astype(qs.dtype)
        key = rotate(kv)
        ks[place] = jnp.where(low_head, key, pltpu.roll(key, HD, 1)).astype(ks.dtype)
        v0[place] = jnp.where(low_head, pltpu.roll(kv, HD, 1), 1.0).astype(v0.dtype)
        v1[place] = jnp.where(low_head, 1.0, kv).astype(v1.dtype)

    def o_copy(block):
        return pltpu.make_async_remote_copy(
            src_ref=ctx.at[block],
            dst_ref=out_ref.at[:, q_cols],
            send_sem=os_sem.at[block],
            recv_sem=or_sem.at[me],
            device_id=dev(dp, block),
            device_id_type=MESH,
        )

    low_tok = lax.broadcasted_iota(jnp.int32, (tok, LANES), 1) < HD
    for block in reversed(range(n_seq)):
        low, high = key_range(block)
        place = slice(block * tok, (block + 1) * tok)
        allowed = bias[block, :, :high - low] > 0.5
        outs = []
        for head, values in ((0, v0), (1, v1)):
            scores = lax.dot_general(
                qs[head, place], ks[low:high], (((1,), (1,)), ((), ())),
                preferred_element_type=jnp.float32,
            )
            scores = jnp.where(allowed, scores, NEG_FILL)
            highest = jnp.max(scores, axis=-1, keepdims=True)
            expons = jnp.exp(scores - highest).astype(values.dtype)
            outs.append(jnp.dot(expons, values[low:high], preferred_element_type=jnp.float32))
        mixed = jnp.where(low_tok, outs[0], outs[1])
        totals = pltpu.roll(jnp.where(low_tok, outs[1], outs[0]), HD, 1)
        ctx[block] = (mixed / totals).astype(ctx.dtype)

        @pl.when(me != block)
        def _():
            o_copy(block).start()

        @pl.when(me == block)
        def _():
            out_ref[:, q_cols] = ctx[block]

    for step in range(1, n_seq):
        source = (me + step) % n_seq
        cols = pl.ds(pl.multiple_of(source * LANES, LANES), LANES)
        pltpu.make_async_remote_copy(
            src_ref=ctx.at[0], dst_ref=out_ref.at[:, cols], send_sem=os_sem.at[0],
            recv_sem=or_sem.at[source], device_id=dev(dp, source), device_id_type=MESH,
        ).wait_recv()

    for block in range(n_seq):
        @pl.when(me != block)
        def _():
            o_copy(block).wait_send()
    for piece in range(PIECES):
        h_to_mate(piece).wait_send()
        for step in range(1, n_x):
            h_to_x(step, piece).wait_send()
            h_forward(step, piece).wait_send()
    for part in range(PARTS):
        send_own(part, wait_send)
        for d in range(1, n_z):
            @pl.when(z >= d)
            def _():
                @pl.when(has_right)
                def _():
                    w_copy(dp - d * INNER, part, 1, right).wait_send()

                w_copy(dp - d * INNER, part, 2, across).wait_send()

            @pl.when(z + d < n_z)
            def _():
                @pl.when(has_left)
                def _():
                    w_copy(dp + d * INNER, part, 0, left).wait_send()

                w_copy(dp + d * INNER, part, 2, across).wait_send()


def shards(hidden_states, query_weight, key_weight, value_weight, doc_lengths):
    n_dp, n_seq = lax.axis_size("dp"), lax.axis_size("seq")
    tok, depth = hidden_states.shape
    kd = query_weight.shape[0]
    length = tok * n_seq
    docs = doc_lengths.shape[1]
    span = min(length, length // 2 + tok)
    half_type, full = jnp.bfloat16, jnp.float32
    any_spec = pl.BlockSpec(memory_space=pl.ANY)
    dma = pltpu.SemaphoreType.DMA
    n_x = n_seq // CORES
    return pl.pallas_call(
        functools.partial(kernel, n_dp, n_seq, docs),
        out_shape=pltpu.VMEM((tok, query_weight.shape[1]), half_type),
        in_specs=[any_spec] * 5,
        out_specs=pl.BlockSpec(memory_space=pltpu.VMEM),
        scratch_shapes=[
            pltpu.SMEM((1, docs), jnp.int32),
            pltpu.VMEM((n_seq, tok, depth), half_type),
            pltpu.VMEM((length, depth), half_type),
            pltpu.VMEM((depth, 2 * LANES), half_type),
            pltpu.VMEM((kd, LANES), half_type),
            pltpu.VMEM((kd, LANES), half_type),
            pltpu.VMEM((length, LANES), full),
            pltpu.VMEM((length, LANES), full),
            pltpu.VMEM((n_seq, tok, span), full),
            pltpu.VMEM((2, length, LANES), half_type),
            pltpu.VMEM((length, LANES), half_type),
            pltpu.VMEM((length, LANES), half_type),
            pltpu.VMEM((length, LANES), half_type),
            pltpu.VMEM((n_seq, tok, LANES), half_type),
            dma((5,)),
            dma((n_x, PIECES)),
            dma((n_x, PIECES)),
            dma((PIECES,)),
            dma((n_seq, PIECES)),
            dma((3, n_dp, PARTS)),
            dma((n_dp, PARTS)),
            dma((n_seq,)),
            dma((n_seq,)),
        ],
        compiler_params=pltpu.CompilerParams(collective_id=0, has_side_effects=True),
    )(hidden_states, query_weight, key_weight, value_weight, doc_lengths)


def solution(mesh):
    placed = (P(("dp", "seq"), None), P("dp", None), P("dp", None), P("dp", None), P("dp", None))
    return jax.shard_map(
        shards, mesh=mesh, in_specs=placed, out_specs=P(("dp", "seq"), None), check_vma=False
    )
```
